512 devices in a mesh: doc: 16 (over z_lo, y), ctx: 32 (over z_hi, x, core).
Axes of the slice: x: 4, y: 8, z: 8 (z_hi: 4, z_lo: 2; z = z_hi * 2 + z_lo), core: 2. Of those that a mesh axis runs over, the one named last changes fastest.
Arguments:
- queries: bfloat16 [16, 4096, 4096], P('doc', 'ctx'), may hold values from -6 to 6, as said below
- key_heads: bfloat16 [16, 4096, 512], P('doc', 'ctx'), may hold values from -6 to 6, as said below
- value_heads: bfloat16 [16, 4096, 512], P('doc', 'ctx'), may hold values from -6 to 6
- out_grad: bfloat16 [16, 4096, 4096], P('doc', 'ctx'), may hold values from -6 to 6
- log_sums: float32 [16, 32, 4096], P('doc', 'ctx'), as said below
- row_delta: float32 [16, 32, 4096], P('doc', 'ctx'), may hold values from -6 to 6
- doc_start: int32 [16], P('doc'), may hold values from 0 to 2048, as said below
- layer_input: bfloat16 [16, 4096, 8192], P('doc', 'ctx'), may hold values from -6 to 6
- hash_in: int32 [8192], replicated, may hold values from 0 to 255
- hash_out: int32 [4096], P('ctx'), may hold values from 0 to 127
- query_sketch: bfloat16 [4096, 8192], P('doc', 'ctx'), may hold values from -6 to 6
Outputs:
- doc_sketch: float32 [16, 8192], P('doc', 'ctx')
- scores: float32 [16, 4096], P(None, ('doc', 'ctx'))
The draws below stay inside these ranges and needn't reach their ends.
Inputs may be any that keep to these rules, and one draw needn't show every extreme that they name: `queries`: drawn together with key_heads; float values. `key_heads`: drawn together with queries; float values. log_sums[e, h, i] is the log of the sum of exp(logits[i, j]) over the positions j visible to i, for the given queries and key_heads; 0 for rows before doc_start[e]. `doc_start`: some document starts at 0 and some at 2048.
All inputs are finite; a program needn't handle non-finite values.
Results may differ from the reference program's by a relative error of at most 0.024.
Values may be sent and summed in bfloat16 or wider, within the bound.
A program may use at most 128 MiB of HBM per device.

```python
import jax
import jax.numpy as jnp
from jax import lax

D = 8192
HD = 128
HEADS = 32
KVH = 4
K1 = 128
K2 = 64
QUERIES = 4096
DOCS = 16
SEQ = 4096
GROUP = 8
SK = 8192


def make_common(key):
    base = jax.random.fold_in(key, 11)
    key_query, key_key, key_start, key_order = jax.random.split(base, 4)
    query_float = jnp.clip(jax.random.normal(key_query, (DOCS, SEQ, HEADS * HD), jnp.float32), -6.0, 6.0)
    key_float = jnp.clip(jax.random.normal(key_key, (DOCS, SEQ, KVH * HD), jnp.float32), -6.0, 6.0)
    starts = jax.random.randint(key_start, (DOCS,), 0, SEQ // 2 + 1, dtype=jnp.int32)
    order = jax.random.permutation(key_order, DOCS)
    starts = starts.at[order[0]].set(0).at[order[1]].set(SEQ // 2)
    return (query_float.astype(jnp.bfloat16), key_float.astype(jnp.bfloat16), starts.astype(jnp.int32))


def draw_queries(key, part):
    return make_common(key)[0]


def draw_key_heads(key, part):
    return make_common(key)[1]


def draw_doc_start(key, part):
    return make_common(key)[2]


def draw_log_sums(key, part):
    query_all, key_all, starts = make_common(key)
    factor = HD ** (-0.5)
    places = jnp.arange(SEQ, dtype=jnp.int32)

    def one_item(item):
        doc_number = item // HEADS
        head_number = item % HEADS
        query_doc = lax.dynamic_index_in_dim(query_all, doc_number, 0, keepdims=False).reshape(SEQ, HEADS, HD)
        key_doc = lax.dynamic_index_in_dim(key_all, doc_number, 0, keepdims=False).reshape(SEQ, KVH, HD)
        query_head = lax.dynamic_index_in_dim(query_doc, head_number, 1, keepdims=False)
        key_head = lax.dynamic_index_in_dim(key_doc, head_number // GROUP, 1, keepdims=False)
        logits = jnp.dot(query_head, key_head.T, preferred_element_type=jnp.float32) * factor
        first_pos = lax.dynamic_index_in_dim(starts, doc_number, 0, keepdims=False)
        visible = (places[None, :] <= places[:, None]) & (places[None, :] >= first_pos)
        masked = jnp.where(visible, logits, -1e+30)
        top_value = jnp.max(masked, axis=1)
        has_keys = places >= first_pos
        safe_top = jnp.where(has_keys, top_value, 0.0)
        totals = jnp.sum(jnp.where(visible, jnp.exp(logits - safe_top[:, None]), 0.0), axis=1)
        safe_total = jnp.where(has_keys, totals, 1.0)
        return jnp.where(has_keys, safe_top + jnp.log(safe_total), 0.0)
    result = lax.map(one_item, jnp.arange(DOCS * HEADS, dtype=jnp.int32))
    return result.reshape(DOCS, HEADS, SEQ).astype(jnp.float32)


def set_ends(drawn, own_key, smallest, high):
    longest = drawn.shape.index(max(drawn.shape))
    spots = []
    for shift in (0, 1):
        where = [jax.random.randint(jax.random.fold_in(own_key, axis), (), 0, length) for axis, length in enumerate(drawn.shape)]
        where[longest] = (where[longest] + shift) % drawn.shape[longest]
        spots.append(tuple(where))
    return drawn.at[spots[0]].set(smallest).at[spots[1]].set(high)


def shard_levels(own_key, extent, shards, least, high):
    gain = 1.0
    for axis_at, shards_of in shards:
        steps = jax.random.uniform(jax.random.fold_in(jax.random.fold_in(own_key, 6), axis_at), (shards_of,), jnp.float32, least / len(shards), high / len(shards))
        gain = gain * jnp.repeat(jnp.exp(steps), extent[axis_at] // shards_of).reshape((-1,) + (1,) * (len(extent) - 1 - axis_at))
    return gain


def noise(key, dims, deviation, most, shards=(), held_as=jnp.bfloat16):
    loudness = shard_levels(key, dims, shards, -0.22, 0.18) if shards else 1.0
    array = jax.random.normal(key, dims, jnp.float32) * deviation * loudness
    return jnp.minimum(jnp.maximum(array, -most), most).astype(held_as)


def setup_inputs(seed: int = 0) -> dict:
    key_list = jax.random.split(jax.random.key(seed), 12)
    queries = draw_queries(jax.random.fold_in(key_list[11], 71), 0)
    key_heads = draw_key_heads(jax.random.fold_in(key_list[11], 71), 0)
    value_heads = noise(key_list[2], (DOCS, SEQ, KVH * HD), 1.0, 6.0, ((0, 16), (1, 32)))
    out_grad = noise(key_list[3], (DOCS, SEQ, HEADS * HD), 1.0, 6.0, ((0, 16), (1, 32)))
    log_sums = draw_log_sums(jax.random.fold_in(key_list[11], 71), 0)
    row_delta = noise(key_list[5], (DOCS, HEADS, SEQ), 1.0, 6.0, ((0, 16), (1, 32)), jnp.float32)
    doc_start = draw_doc_start(jax.random.fold_in(key_list[11], 71), 0)
    layer_input = noise(key_list[7], (DOCS, SEQ, D), 1.0, 6.0, ((0, 16), (1, 32)))
    hash_in = set_ends(jax.random.randint(key_list[8], (D,), 0, 2 * K1), jax.random.fold_in(key_list[8], 1), 0, (2 * K1) - 1).astype(jnp.int32)
    hash_out = set_ends(jax.random.randint(key_list[9], (HEADS * HD,), 0, 2 * K2), jax.random.fold_in(key_list[9], 1), 0, (2 * K2) - 1).astype(jnp.int32)
    query_sketch = noise(key_list[10], (QUERIES, SK), 1.0, 6.0, ((0, 16), (1, 32)))
    return {"queries": queries, "key_heads": key_heads, "value_heads": value_heads, "out_grad": out_grad, "log_sums": log_sums, "row_delta": row_delta, "doc_start": doc_start, "layer_input": layer_input, "hash_in": hash_in, "hash_out": hash_out, "query_sketch": query_sketch}


def sign_table(codes, buckets):
    levels = jnp.arange(buckets, dtype=jnp.int32)
    plus_part = (codes[..., None] == levels).astype(jnp.float32)
    minus_part = (codes[..., None] == levels + buckets).astype(jnp.float32)
    return plus_part - minus_part


def attend_head(query_head, key_head, value_head, grad_head, log_head, delta_head, first_pos):
    factor = HD ** -0.5
    logits = jnp.dot(query_head, key_head.T, preferred_element_type=jnp.float32) * factor
    places = jnp.arange(SEQ, dtype=jnp.int32)
    visible = (places[None, :] <= places[:, None]) & (places[None, :] >= first_pos)
    weights = jnp.where(visible, jnp.exp(logits - log_head[:, None]), 0.0)
    grad_weights = jnp.dot(grad_head, value_head.T, preferred_element_type=jnp.float32)
    grad_scores = (weights * (grad_weights - delta_head[:, None])).astype(jnp.bfloat16)
    product = jnp.dot(grad_scores, key_head, preferred_element_type=jnp.float32)
    return (product * factor).astype(jnp.bfloat16)


def reference(queries, key_heads, value_heads, out_grad, log_sums, row_delta, doc_start, layer_input, hash_in, hash_out, query_sketch):
    table_in = sign_table(hash_in, K1)
    table_out = sign_table(hash_out.reshape(HEADS, HD), K2)

    def one_document(items):
        query_doc, key_doc, value_doc, grad_doc, log_doc, delta_doc, first_pos, input_doc = items
        query_three = query_doc.reshape(SEQ, HEADS, HD)
        grad_three = grad_doc.reshape(SEQ, HEADS, HD)
        key_three = key_doc.reshape(SEQ, KVH, HD)
        value_three = value_doc.reshape(SEQ, KVH, HD)

        def per_head(head_number):
            group_number = head_number // GROUP
            query_head = lax.dynamic_index_in_dim(query_three, head_number, 1, keepdims=False)
            grad_head = lax.dynamic_index_in_dim(grad_three, head_number, 1, keepdims=False)
            key_head = lax.dynamic_index_in_dim(key_three, group_number, 1, keepdims=False)
            value_head = lax.dynamic_index_in_dim(value_three, group_number, 1, keepdims=False)
            log_head = lax.dynamic_index_in_dim(log_doc, head_number, 0, keepdims=False)
            delta_head = lax.dynamic_index_in_dim(delta_doc, head_number, 0, keepdims=False)
            return attend_head(query_head, key_head, value_head, grad_head, log_head, delta_head, first_pos)

        grad_query = lax.map(per_head, jnp.arange(HEADS, dtype=jnp.int32))
        hashed_grads = jnp.einsum("hsd,hdb->shb", grad_query.astype(jnp.float32), table_out,
                                  precision=lax.Precision.HIGHEST).astype(jnp.bfloat16)
        hashed_inputs = jnp.dot(input_doc, table_in.astype(jnp.bfloat16),
                                preferred_element_type=jnp.float32).astype(jnp.bfloat16)
        sketch = jnp.einsum("sa,shb->ab", hashed_inputs.astype(jnp.float32), hashed_grads.astype(jnp.float32),
                            precision=lax.Precision.HIGHEST)
        return (sketch * (SEQ * D // K1) ** -0.5).reshape(SK)

    doc_sketch = lax.map(one_document, (queries, key_heads, value_heads, out_grad, log_sums, row_delta, doc_start, layer_input))
    scores = jnp.dot(doc_sketch, query_sketch.astype(jnp.float32).T, precision=lax.Precision.HIGHEST) * SK ** -0.5
    return doc_sketch, scores
```

```python
import functools

import jax
import jax.numpy as jnp
from jax import lax
from jax.experimental import pallas as pl
from jax.experimental.pallas import tpu as pltpu
from jax.sharding import PartitionSpec as P

HD = 128
K1 = 128
K2 = 64
SEQ = 4096
DIM = 8192
DOCS = 16
RANKS = 32
ROWS = 128
BLOCK = 256
PLANE = 1024
LOG2E = 1.4426950408889634
SCORE = HD**-0.5
NEG = -1e30
NT = (((1,), (1,)), ((), ()))
TN = (((0,), (0,)), ((), ()))
F32 = jnp.float32
BF16 = jnp.bfloat16


def kernel(
    q_hbm, k_hbm, v_hbm, do_hbm, lse_ref, dl_ref, start_ref, x_hbm, hin_ref, hout_ref, qs_ref,
    sketch_out, scores_out,
    qb, dob, kv, acc, xb, ld, msg, hit_own, hit, bias, part, rs1, sk_send, sk_all, part2, rs2,
    xsem, lsem, msg_ss, msg_rs, kx_ss, kx_rs, q_ss, q_rs, do_ss, do_rs, z_ss, z_rs, s_ss, s_rs,
    hi_ss, hi_rs, r1_ss, r1_rs, ag_ss, ag_rs, r2_ss, r2_rs,
):
    doc = lax.axis_index("doc")
    me = lax.axis_index("ctx")
    zz = me // 8
    xx = (me // 2) % 4
    cc = me % 2
    base = zz * 8
    in_plane = me % 8

    def remote(src, dst, ss, rs, peer):
        return pltpu.make_async_remote_copy(
            src_ref=src, dst_ref=dst, send_sem=ss, recv_sem=rs,
            device_id={"ctx": peer}, device_id_type=pl.DeviceIdType.MESH,
        )

    barrier = pltpu.get_barrier_semaphore()

    def greet(i, _):
        pl.semaphore_signal(
            barrier, inc=1, device_id={"ctx": (me + i) % RANKS},
            device_id_type=pl.DeviceIdType.MESH,
        )
        return 0

    lax.fori_loop(1, RANKS, greet, 0)

    def greet_doc(i, _):
        pl.semaphore_signal(
            barrier, inc=1, device_id={"doc": (doc + i) % DOCS},
            device_id_type=pl.DeviceIdType.MESH,
        )
        return 0

    lax.fori_loop(1, DOCS, greet_doc, 0)

    x_copy = pltpu.make_async_copy(x_hbm.at[0], xb, xsem)
    x_copy.start()
    ld[0] = lse_ref[...] * LOG2E
    ld[1] = dl_ref[...]
    ld[2] = jnp.broadcast_to(hout_ref[...].astype(F32), (32, 128))

    pl.semaphore_wait(barrier, RANKS - 1 + DOCS - 1)

    def kx(i):
        to = (in_plane + i) % 8
        lanes = pl.ds(pl.multiple_of((to // 2) * HD, HD), HD)
        rows = pl.ds(pl.multiple_of(me * ROWS, ROWS), ROWS)
        return to, (
            (k_hbm.at[0, :, lanes], kv.at[0, rows, :]),
            (v_hbm.at[0, :, lanes], kv.at[1, rows, :]),
        )

    def kx_start(i, _):
        to, pairs = kx(i)
        for src, dst in pairs:
            remote(src, dst, kx_ss, kx_rs, base + to).start()
        return 0

    lax.fori_loop(1, 8, kx_start, 0)
    for src, dst in kx(0)[1]:
        pltpu.make_async_copy(src, dst, kx_rs).start()

    own_head = (me // 8) * 2 + (me % 8) // 4
    slot = me % 4

    def msg_pair(i):
        rows = pl.ds(pl.multiple_of(i * 8, 8), 8)
        return ld.at[:, rows, :], msg.at[slot]

    def msg_each(i, go):
        src, dst = msg_pair(i)
        peer = i * 8 + own_head

        @pl.when(peer != me)
        def _():
            go(remote(src, dst, msg_ss.at[i], msg_rs.at[slot], peer))

        return src, dst, peer

    def msg_start(i, _):
        src, dst, peer = msg_each(i, lambda c: c.start())

        @pl.when(peer == me)
        def _():
            pltpu.make_async_copy(src, dst, msg_rs.at[slot]).start()

        return 0

    lax.fori_loop(0, 4, msg_start, 0)

    def qx(i):
        to = (in_plane + i) % 8
        lanes = pl.ds(pl.multiple_of(to * 512, 512), 512)
        rows = pl.ds(pl.multiple_of(cc * ROWS, ROWS), ROWS)
        return to, (q_hbm.at[0, :, lanes], qb.at[xx, rows, :]), (
            do_hbm.at[0, :, lanes],
            dob.at[xx, rows, :],
        )

    def qx_copy(i):
        to, a, b = qx(i)
        return (
            remote(*a, q_ss.at[i], q_rs.at[xx], base + to),
            remote(*b, do_ss.at[i], do_rs.at[xx], base + to),
        )

    for src, dst, sem in ((*qx(0)[1], q_rs.at[xx]), (*qx(0)[2], do_rs.at[xx])):
        pltpu.make_async_copy(src, dst, sem).start()

    def qx_order(n):
        near = jnp.where(n < 3, 2, jnp.where(n < 5, 6, 4))
        other = near + ((n + 1) % 2) * (1 - 2 * cc)
        return jnp.where(n == 0, (1 - 2 * cc) % 8, other % 8)

    def qx_start(n, _):
        a, b = qx_copy(qx_order(n))
        a.start()
        b.start()
        return 0

    lax.fori_loop(0, 7, qx_start, 0)

    x_copy.wait()
    bucket_of = lax.broadcasted_iota(jnp.int32, (K1, 1024), 0)

    def hash_step(j, total):
        cols = pl.ds(pl.multiple_of(j * 1024, 1024), 1024)
        codes = hin_ref[:, cols]
        low = codes < K1
        bucket = jnp.where(low, codes, codes - K1)
        sign = jnp.where(low, 1.0, -1.0)
        table = jnp.where(bucket_of == bucket, sign, 0.0).astype(BF16)
        return total + lax.dot_general(table, xb[:, cols], NT, preferred_element_type=F32)

    hit_own[...] = lax.fori_loop(0, DIM // 1024, hash_step, jnp.zeros((K1, ROWS), F32)).astype(BF16)

    hit_lanes = pl.ds(pl.multiple_of(in_plane * ROWS, ROWS), ROWS)

    def hit_copy(i):
        return remote(hit_own, hit.at[:, hit_lanes], hi_ss.at[i], hi_rs, base + (in_plane + i) % 8)

    def hit_start(i, _):
        hit_copy(i).start()
        return 0

    lax.fori_loop(1, 8, hit_start, 0)
    pltpu.make_async_copy(hit_own, hit.at[:, hit_lanes], hi_rs).start()

    bias[...] = jnp.where(
        lax.broadcasted_iota(jnp.int32, (SEQ, HD), 0) >= start_ref[0], 0.0, NEG
    ).astype(F32)
    acc[...] = jnp.zeros_like(acc)

    own_rows = pl.ds(pl.multiple_of(zz * PLANE, PLANE), PLANE)
    pltpu.make_async_copy(kv.at[:, own_rows, :], kv.at[:, own_rows, :], kx_rs).wait()

    def half(plane, core):
        return kv.at[:, pl.ds(pl.multiple_of(plane * PLANE + core * 512, 512), 512), :]

    def z_copy(plane, to, s):
        return remote(half(plane, cc), half(plane, cc), z_ss.at[s], z_rs.at[plane], to * 8 + in_plane)

    def s_copy(plane):
        return remote(
            half(plane, cc), half(plane, cc), s_ss.at[plane], s_rs.at[plane], me + 1 - 2 * cc
        )

    @pl.when(zz < 3)
    def _():
        z_copy(zz, zz + 1, 0).start()

    @pl.when(zz == 0)
    def _():
        z_copy(0, 3, 1).start()

    def z_arrive(plane):
        pltpu.make_async_copy(half(plane, cc), half(plane, cc), z_rs.at[plane]).wait()
        s_copy(plane).start()

    def s_arrive(plane):
        pltpu.make_async_copy(
            half(plane, 1 - cc), half(plane, 1 - cc), s_rs.at[plane]
        ).wait()

    def front(rb, h, kk, vv):
        head = slice(h * HD, (h + 1) * HD)
        s = lax.dot_general(kk, qb[rb, :, head], NT, preferred_element_type=F32)
        gw = lax.dot_general(vv, dob[rb, :, head], NT, preferred_element_type=F32)
        return s, gw

    def back(rb, h, kk, low, s, gw, diagonal):
        count = kk.shape[0]
        lse = jnp.concatenate(
            [msg[h, 0, pl.ds(2 * rb, 1), :], msg[h, 0, pl.ds(2 * rb + 1, 1), :]], axis=1
        )
        delta = jnp.concatenate(
            [msg[h, 1, pl.ds(2 * rb, 1), :], msg[h, 1, pl.ds(2 * rb + 1, 1), :]], axis=1
        )
        x = s * (SCORE * LOG2E) - lse + jnp.concatenate([low, low], axis=1)
        p = jnp.exp2(x)
        if diagonal:
            seen = lax.broadcasted_iota(jnp.int32, (BLOCK, BLOCK), 0) <= lax.broadcasted_iota(
                jnp.int32, (BLOCK, BLOCK), 1
            )
            last = jnp.where(seen, p[count - BLOCK :], 0.0)
            p = last if count == BLOCK else jnp.concatenate([p[: count - BLOCK], last], axis=0)
        ds = (p * (gw - delta)).astype(BF16)
        r = lax.dot_general(kk, ds, TN, preferred_element_type=F32)
        rows = pl.ds(pl.multiple_of((rb * 4 + h) * HD, HD), HD)
        acc[rows, :] += r

    def heads(rb, lo, count, diagonal):
        keys = pl.ds(pl.multiple_of(lo, BLOCK), count)
        kk = kv[0, keys, :]
        vv = kv[1, keys, :]
        low = bias[keys, :]
        now = front(rb, 0, kk, vv)
        for h in range(4):
            later = front(rb, h + 1, kk, vv) if h < 3 else None
            back(rb, h, kk, low, *now, diagonal)
            now = later

    def order(i):
        return (xx + jnp.where(i == 2, 3, jnp.where(i == 3, 2, i))) % 4

    def diag_step(i, _):
        rb = order(i)
        rows = qb.at[rb]
        pltpu.make_async_copy(rows, rows, q_rs.at[rb]).wait()
        rows = dob.at[rb]
        pltpu.make_async_copy(rows, rows, do_rs.at[rb]).wait()
        for r in range(4):

            @pl.when(rb == r)
            def _():
                heads(r, zz * PLANE, (r + 1) * BLOCK, True)

        return 0

    def plane_steps(plane, first, last):
        def step(i, _):
            heads(order(i), plane * PLANE, PLANE, False)
            return 0

        lax.fori_loop(first, last, step, 0)

    def msg_wait(i, _):
        pltpu.make_async_copy(msg.at[i], msg.at[i], msg_rs.at[i]).wait()
        return 0

    lax.fori_loop(0, 4, msg_wait, 0)

    lax.fori_loop(0, 3, diag_step, 0)

    @pl.when(zz >= 1)
    def _():
        z_arrive(zz - 1)

        @pl.when(zz < 3)
        def _():
            z_copy(zz - 1, zz + 1, 1).start()

    @pl.when(zz == 3)
    def _():
        z_arrive(0)

    @pl.when(zz >= 1)
    def _():
        s_arrive(zz - 1)
        plane_steps(zz - 1, 0, 3)

    @pl.when(zz == 3)
    def _():
        s_arrive(0)
        plane_steps(0, 0, 3)

    lax.fori_loop(3, 4, diag_step, 0)

    @pl.when(zz >= 1)
    def _():
        plane_steps(zz - 1, 3, 4)

    @pl.when(zz == 3)
    def _():
        z_arrive(1)
        plane_steps(0, 3, 4)
        s_arrive(1)
        plane_steps(1, 0, 4)

    @pl.when(zz == 2)
    def _():
        z_arrive(0)
        s_arrive(0)
        plane_steps(0, 0, 4)

    pltpu.make_async_copy(hit, hit, hi_rs).wait()
    feature_bucket = lax.broadcasted_iota(jnp.int32, (K2, HD), 0).astype(F32)
    pieces = []
    for h in range(4):
        codes = msg[h, 2, 0:1, :]
        low = codes < K2
        bucket = jnp.where(low, codes, codes - K2)
        sign = jnp.where(low, 1.0, -1.0)
        pieces.append(jnp.where(feature_bucket == bucket, sign, 0.0).astype(BF16))
    table_out = jnp.concatenate(pieces, axis=1)
    total = jnp.zeros((K1, 2 * K2), F32)
    for rb in range(4):
        gq = (acc[rb * 512 : (rb + 1) * 512, :] * SCORE).astype(BF16)
        hg = jnp.dot(table_out, gq, preferred_element_type=F32)
        high = hg.astype(BF16)
        rest = (hg - high.astype(F32)).astype(BF16)
        both = jnp.concatenate([high, rest], axis=0)
        total += lax.dot_general(
            hit[:, rb * BLOCK : (rb + 1) * BLOCK], both, NT, preferred_element_type=F32
        )
    part[...] = total

    def r1_start(i, _):
        to = (me + i) % RANKS
        rows = pl.ds(pl.multiple_of((to // 2) * 8, 8), 8)
        remote(part.at[rows, :], rs1.at[me], r1_ss, r1_rs, to).start()
        return 0

    lax.fori_loop(1, RANKS, r1_start, 0)
    mine = pl.ds(pl.multiple_of((me // 2) * 8, 8), 8)
    pltpu.make_async_copy(part.at[mine, :], rs1.at[me], r1_rs).start()
    pltpu.make_async_copy(rs1, rs1, r1_rs).wait()
    summed = jnp.sum(rs1[...], axis=0)
    summed = (summed + pltpu.roll(summed, K2, 1)) * (SEQ * DIM // K1) ** -0.5
    summed = jnp.where(cc == 0, summed, pltpu.roll(summed, 4, 0))
    left = lax.broadcasted_iota(jnp.int32, (1, HD), 1) < K2
    first = jnp.where(left, summed[0:1, :], summed[1:2, :])
    second = jnp.where(left, summed[2:3, :], summed[3:4, :])
    sketch_out[...] = jnp.concatenate([first, second], axis=1)
    sk_send[...] = jnp.concatenate([first, second, jnp.zeros((6, HD), F32)], axis=0)

    def ag_copy(i):
        return pltpu.make_async_remote_copy(
            src_ref=sk_send, dst_ref=sk_all.at[doc], send_sem=ag_ss, recv_sem=ag_rs,
            device_id={"doc": (doc + i) % DOCS}, device_id_type=pl.DeviceIdType.MESH,
        )

    def ag_start(i, _):
        ag_copy(i).start()
        return 0

    lax.fori_loop(1, DOCS, ag_start, 0)
    pltpu.make_async_copy(sk_send, sk_all.at[doc], ag_rs).start()
    pltpu.make_async_copy(sk_all, sk_all, ag_rs).wait()

    flat = sk_all[...].reshape(DOCS * 8, HD)
    stored = qs_ref[...].astype(F32)
    high = lax.Precision.HIGHEST
    even = lax.dot_general(stored[:, :HD], flat, NT, precision=high, preferred_element_type=F32)
    odd = lax.dot_general(stored[:, HD:], flat, NT, precision=high, preferred_element_type=F32)
    part2[...] = even + pltpu.roll(odd, HD - 1, 1)

    def r2_start(i, _):
        to = (me + i) % RANKS
        rows = pl.ds(pl.multiple_of(to * 8, 8), 8)
        remote(part2.at[rows, :], rs2.at[me], r2_ss, r2_rs, to).start()
        return 0

    lax.fori_loop(1, RANKS, r2_start, 0)
    mine = pl.ds(pl.multiple_of(me * 8, 8), 8)
    pltpu.make_async_copy(part2.at[mine, :], rs2.at[me], r2_rs).start()
    pltpu.make_async_copy(rs2, rs2, r2_rs).wait()
    totals = jnp.sum(rs2[...], axis=0) * (K1 * K2) ** -0.5
    pick = (
        lax.broadcasted_iota(jnp.int32, (DOCS, HD), 1)
        == 8 * lax.broadcasted_iota(jnp.int32, (DOCS, HD), 0)
    ).astype(F32)
    scores_out[...] = lax.dot_general(
        pick, totals, NT, precision=high, preferred_element_type=F32
    )

    for src in (kv.at[:, 0:896, :],):
        pltpu.make_async_copy(src, src, kx_ss).wait()

    def msg_done(i, _):
        msg_each(i, lambda c: c.wait_send())
        return 0

    lax.fori_loop(0, 4, msg_done, 0)

    def qx_done(i, _):
        a, b = qx_copy(i)
        a.wait_send()
        b.wait_send()
        hit_copy(i).wait_send()
        return 0

    lax.fori_loop(1, 8, qx_done, 0)

    @pl.when(zz < 3)
    def _():
        z_copy(zz, zz + 1, 0).wait_send()

    @pl.when(zz == 0)
    def _():
        z_copy(0, 3, 1).wait_send()

    @pl.when((zz == 1) | (zz == 2))
    def _():
        z_copy(zz - 1, zz + 1, 1).wait_send()

    def s_done(i, _):
        s_copy(i).wait_send()
        return 0

    lax.fori_loop(0, zz, s_done, 0)
    pltpu.make_async_copy(rs1.at[1:], rs1.at[1:], r1_ss).wait()
    pltpu.make_async_copy(sk_all.at[1:], sk_all.at[1:], ag_ss).wait()
    pltpu.make_async_copy(rs2.at[1:], rs2.at[1:], r2_ss).wait()


def local(
    queries, key_heads, value_heads, out_grad, log_sums, row_delta, doc_start,
    layer_input, hash_in, hash_out, query_sketch,
):
    hbm = pl.BlockSpec(memory_space=pl.ANY)
    vmem = pl.BlockSpec(memory_space=pltpu.VMEM)
    smem = pl.BlockSpec(memory_space=pltpu.SMEM)
    dma = pltpu.SemaphoreType.DMA
    return pl.pallas_call(
        kernel,
        out_shape=(
            jax.ShapeDtypeStruct((1, 256), F32),
            jax.ShapeDtypeStruct((DOCS, 8), F32),
        ),
        in_specs=[hbm, hbm, hbm, hbm, vmem, vmem, smem, hbm, vmem, vmem, vmem],
        out_specs=(vmem, vmem),
        scratch_shapes=[
            pltpu.VMEM((4, BLOCK, 512), BF16),
            pltpu.VMEM((4, BLOCK, 512), BF16),
            pltpu.VMEM((2, SEQ, HD), BF16),
            pltpu.VMEM((2048, BLOCK), F32),
            pltpu.VMEM((ROWS, DIM), BF16),
            pltpu.VMEM((3, 32, HD), F32),
            pltpu.VMEM((4, 3, 8, HD), F32),
            pltpu.VMEM((K1, ROWS), BF16),
            pltpu.VMEM((K1, PLANE), BF16),
            pltpu.VMEM((SEQ, HD), F32),
            pltpu.VMEM((K1, 2 * K2), F32),
            pltpu.VMEM((RANKS, 8, HD), F32),
            pltpu.VMEM((8, HD), F32),
            pltpu.VMEM((DOCS, 8, HD), F32),
            pltpu.VMEM((256, HD), F32),
            pltpu.VMEM((RANKS, 8, HD), F32),
            dma, dma,
            dma((4,)), dma((4,)),
            dma, dma,
            dma((8,)), dma((4,)), dma((8,)), dma((4,)),
            dma((2,)), dma((4,)), dma((4,)), dma((4,)),
            dma((8,)), dma,
            dma, dma, dma, dma, dma, dma,
        ],
        compiler_params=pltpu.CompilerParams(
            collective_id=0, has_side_effects=True, vmem_limit_bytes=56 * 2**20
        ),
    )(
        queries, key_heads, value_heads, out_grad,
        log_sums.reshape(32, 128), row_delta.reshape(32, 128), doc_start, layer_input,
        hash_in.reshape(1, DIM), hash_out.reshape(1, HD), query_sketch,
    )


def solution(mesh):
    return jax.shard_map(
        local,
        mesh=mesh,
        in_specs=(
            P("doc", "ctx", None),
            P("doc", "ctx", None),
            P("doc", "ctx", None),
            P("doc", "ctx", None),
            P("doc", "ctx", None),
            P("doc", "ctx", None),
            P("doc"),
            P("doc", "ctx", None),
            P(),
            P("ctx"),
            P("doc", "ctx"),
        ),
        out_specs=(P("doc", "ctx"), P(None, ("doc", "ctx"))),
        check_vma=False,
    )
```

```python
import functools

import jax
import jax.numpy as jnp
from jax import lax
from jax.experimental import pallas as pl
from jax.experimental.pallas import tpu as pltpu
from jax.sharding import PartitionSpec as P

HD = 128
K1 = 128
K2 = 64
SEQ = 4096
DIM = 8192
DOCS = 16
RANKS = 32
ROWS = 128
BLOCK = 256
PLANE = 1024
LOG2E = 1.4426950408889634
SCORE = HD**-0.5
NEG = -1e30
NT = (((1,), (1,)), ((), ()))
TN = (((0,), (0,)), ((), ()))
F32 = jnp.float32
BF16 = jnp.bfloat16


def wrap(value, count):
    return jnp.where(value >= count, value - count, value)


def kernel(
    q_hbm, k_hbm, v_hbm, do_hbm, lse_ref, dl_ref, start_ref, x_hbm, hin_ref, hout_ref, qs_ref,
    sketch_out, scores_out,
    qd, kv, acc, xb, ld, msg, hit_own, hit, bias, part, rs1, sk_send, sk_all, part2, rs2,
    xsem, msg_ss, msg_rs, kx_ss, kx_rs, q_ss, q_rs, z_ss, z_rs, s_ss, s_rs,
    hi_ss, hi_rs, hs_ss, hs_rs, r1_ss, r1_rs, ag_ss, ag_rs, r2_ss, r2_rs,
):
    doc = lax.axis_index("doc")
    me = lax.axis_index("ctx")
    zz = me // 8
    in_plane = me - 8 * zz
    xx = in_plane // 2
    cc = in_plane - 2 * xx
    base = zz * 8
    sibling = me + 1 - 2 * cc

    def remote(src, dst, ss, rs, peer):
        return pltpu.make_async_remote_copy(
            src_ref=src, dst_ref=dst, send_sem=ss, recv_sem=rs,
            device_id={"ctx": peer}, device_id_type=pl.DeviceIdType.MESH,
        )

    def done(ref, sem):
        pltpu.make_async_copy(ref, ref, sem).wait()

    barrier = pltpu.get_barrier_semaphore()
    for i in range(1, RANKS):
        pl.semaphore_signal(
            barrier, inc=1, device_id={"ctx": wrap(me + i, RANKS)},
            device_id_type=pl.DeviceIdType.MESH,
        )
    for i in range(1, DOCS):
        pl.semaphore_signal(
            barrier, inc=1, device_id={"doc": wrap(doc + i, DOCS)},
            device_id_type=pl.DeviceIdType.MESH,
        )
    x_copy = pltpu.make_async_copy(x_hbm.at[0], xb, xsem)
    x_copy.start()
    ld[0] = lse_ref[...] * LOG2E
    ld[1] = dl_ref[...]
    ld[2] = jnp.broadcast_to(hout_ref[...].astype(F32), (32, 128))
    pl.semaphore_wait(barrier, RANKS - 1 + DOCS - 1)

    def half(plane, core):
        return kv.at[:, pl.ds(plane * 4, 4), core]

    for dx in (1, 3, 2, 0):
        to = wrap(xx + dx, 4)
        lanes = pl.ds(pl.multiple_of(to * HD, HD), HD)
        for n, src in enumerate((k_hbm, v_hbm)):
            src = src.at[0, :, lanes]
            dst = kv.at[n, zz * 4 + xx, cc]
            if dx == 0:
                pltpu.make_async_copy(src, dst, kx_rs).start()
            else:
                remote(src, dst, kx_ss, kx_rs, base + 2 * to + cc).start()

    def z_each(go):
        @pl.when(zz < 3)
        def _():
            go(zz + 1, 0)

        @pl.when(zz == 0)
        def _():
            go(3, 1)

    def z_first(to, s):
        lanes = pl.ds(pl.multiple_of(xx * HD, HD), HD)
        for n, src in enumerate((k_hbm, v_hbm)):
            dst = kv.at[n, zz * 4 + xx, cc]
            remote(src.at[0, :, lanes], dst, z_ss.at[s], z_rs.at[zz], to * 8 + in_plane).start()

    z_each(z_first)

    rows = pl.ds(pl.multiple_of(cc * ROWS, ROWS), ROWS)

    def q_send(slot, dx, other):
        to = 2 * wrap(xx + dx, 4) + (1 - cc if other else cc)
        lanes = pl.ds(pl.multiple_of(to * 512, 512), 512)
        for n, src in enumerate((q_hbm, do_hbm)):
            src = src.at[0, :, lanes]
            dst = qd.at[n, xx, rows, :]
            if slot == 7:
                pltpu.make_async_copy(src, dst, q_rs.at[xx]).start()
            else:
                remote(src, dst, q_ss.at[slot], q_rs.at[xx], base + to).start()

    def q_left(slot):
        done(qd.at[:, 0, 0:ROWS, :], q_ss.at[slot])

    for slot, dx, other in ((0, 0, 1), (1, 1, 0), (2, 3, 0), (3, 1, 1), (4, 3, 1), (7, 0, 0)):
        q_send(slot, dx, other)

    own_head = zz * 2 + in_plane // 4
    head_slot = in_plane - 4 * (in_plane // 4)

    def msg_each(i, go):
        src, dst = ld.at[:, i * 8 : i * 8 + 8, :], msg.at[head_slot]
        peer = i * 8 + own_head

        @pl.when(peer != me)
        def _():
            go(remote(src, dst, msg_ss.at[i], msg_rs.at[head_slot], peer))

        return src, dst, peer

    for i in range(4):
        src, dst, peer = msg_each(i, lambda c: c.start())

        @pl.when(peer == me)
        def _():
            pltpu.make_async_copy(src, dst, msg_rs.at[head_slot]).start()

    def s_copy(plane):
        return remote(half(plane, cc), half(plane, cc), s_ss.at[plane], s_rs.at[plane], sibling)

    def z_block(dx, to, s):
        block = kv.at[:, zz * 4 + wrap(xx + dx, 4), cc]
        return remote(block, block, z_ss.at[s], z_rs.at[zz], to * 8 + in_plane)

    def z_send(to, s):
        for dx in (1, 3, 2):
            z_block(dx, to, s).start()

    done(half(zz, cc), kx_rs)
    z_each(z_send)
    s_copy(zz).start()

    def z_whole(plane, to, s):
        return remote(half(plane, cc), half(plane, cc), z_ss.at[s], z_rs.at[plane], to * 8 + in_plane)

    def z_arrive(plane):
        done(half(plane, cc), z_rs.at[plane])
        s_copy(plane).start()

    def s_arrive(plane):
        done(half(plane, 1 - cc), s_rs.at[plane])

    bias[...] = jnp.where(
        lax.broadcasted_iota(jnp.int32, (SEQ, HD), 0) >= start_ref[0], 0.0, NEG
    ).astype(F32)
    acc[...] = jnp.zeros_like(acc)

    x_copy.wait()
    bucket_of = lax.broadcasted_iota(jnp.int32, (K1, 1024), 0)

    def hash_step(j, total):
        cols = pl.ds(pl.multiple_of(j * 1024, 1024), 1024)
        codes = hin_ref[:, cols]
        low = codes < K1
        bucket = jnp.where(low, codes, codes - K1)
        sign = jnp.where(low, 1.0, -1.0)
        table = jnp.where(bucket_of == bucket, sign, 0.0).astype(BF16)
        return total + lax.dot_general(table, xb[:, cols], NT, preferred_element_type=F32)

    hit_own[...] = lax.fori_loop(0, DIM // 1024, hash_step, jnp.zeros((K1, ROWS), F32)).astype(BF16)

    def hit_copy(dx):
        to = base + 2 * wrap(xx + dx, 4) + cc
        return remote(hit_own, hit.at[xx, cc], hi_ss.at[dx], hi_rs, to)

    def hit_side():
        return remote(hit.at[:, cc], hit.at[:, cc], hs_ss, hs_rs, sibling)

    def front(rb, h, kk, vv):
        head = slice(h * HD, (h + 1) * HD)
        s = lax.dot_general(kk, qd[0, rb, :, head], NT, preferred_element_type=F32)
        gw = lax.dot_general(vv, qd[1, rb, :, head], NT, preferred_element_type=F32)
        return s, gw

    def back(rb, h, kk, low, s, gw, diagonal):
        count = kk.shape[0]
        lse = jnp.concatenate(
            [msg[h, 0, pl.ds(2 * rb, 1), :], msg[h, 0, pl.ds(2 * rb + 1, 1), :]], axis=1
        )
        delta = jnp.concatenate(
            [msg[h, 1, pl.ds(2 * rb, 1), :], msg[h, 1, pl.ds(2 * rb + 1, 1), :]], axis=1
        )
        x = s * (SCORE * LOG2E) - lse + jnp.concatenate([low, low], axis=1)
        p = jnp.exp2(x)
        if diagonal:
            seen = lax.broadcasted_iota(jnp.int32, (BLOCK, BLOCK), 0) <= lax.broadcasted_iota(
                jnp.int32, (BLOCK, BLOCK), 1
            )
            last = jnp.where(seen, p[count - BLOCK :], 0.0)
            p = last if count == BLOCK else jnp.concatenate([p[: count - BLOCK], last], axis=0)
        ds = (p * (gw - delta)).astype(BF16)
        r = lax.dot_general(kk, ds, TN, preferred_element_type=F32)
        rows = pl.ds(pl.multiple_of((rb * 4 + h) * HD, HD), HD)
        acc[rows, :] += r

    def heads(rb, plane, chips, diagonal):
        count = chips * BLOCK
        blocks = pl.ds(plane * 4, chips)
        kk = kv[0, blocks].reshape(count, HD)
        vv = kv[1, blocks].reshape(count, HD)
        low = bias[pl.ds(pl.multiple_of(plane * PLANE, PLANE), count), :]
        now = front(rb, 0, kk, vv)
        for h in range(4):
            later = front(rb, h + 1, kk, vv) if h < 3 else None
            back(rb, h, kk, low, *now, diagonal)
            now = later

    def order(i):
        return wrap(xx + jnp.where(i == 2, 3, jnp.where(i == 3, 2, i)), 4)

    def diag_step(i, _):
        rb = order(i)
        done(qd.at[:, rb], q_rs.at[rb])
        for r in range(4):

            @pl.when(rb == r)
            def _():
                heads(r, zz, r + 1, True)

        return 0

    def plane_steps(plane, chips, first, last):
        def step(i, _):
            heads(order(i), plane, chips, False)
            return 0

        lax.fori_loop(first, last, step, 0)

    for i in range(4):
        done(msg.at[i], msg_rs.at[i])
    s_arrive(zz)

    lax.fori_loop(0, 1, diag_step, 0)

    @pl.when(zz == 1)
    def _():
        done(half(0, 0), z_ss.at[0])
        z_whole(1, 3, 0).start()

    for slot in (1, 2, 3, 4):
        q_left(slot)
    q_send(5, 2, 0)
    q_send(6, 2, 1)
    lax.fori_loop(1, 3, diag_step, 0)

    @pl.when(zz >= 1)
    def _():
        z_arrive(zz - 1)

    @pl.when(zz == 1)
    def _():
        z_whole(0, 2, 1).start()

    @pl.when(zz == 3)
    def _():
        z_arrive(0)

    @pl.when(zz >= 1)
    def _():
        s_arrive(zz - 1)
        plane_steps(zz - 1, 4, 0, 3)

    @pl.when(zz == 3)
    def _():
        s_arrive(0)
        plane_steps(0, 4, 0, 3)

    lax.fori_loop(3, 4, diag_step, 0)
    for dx in range(1, 4):
        hit_copy(dx).start()
    pltpu.make_async_copy(hit_own, hit.at[xx, cc], hi_rs).start()

    @pl.when(zz >= 1)
    def _():
        plane_steps(zz - 1, 4, 3, 4)

    @pl.when(zz == 3)
    def _():
        z_arrive(1)
        plane_steps(0, 4, 3, 4)

    done(hit.at[:, cc], hi_rs)
    hit_side().start()

    @pl.when(zz == 3)
    def _():
        s_arrive(1)
        plane_steps(1, 4, 0, 4)

    @pl.when(zz == 2)
    def _():
        z_arrive(0)
        s_arrive(0)
        plane_steps(0, 4, 0, 4)

    done(hit.at[:, 1 - cc], hs_rs)
    feature_bucket = lax.broadcasted_iota(jnp.int32, (K2, HD), 0).astype(F32)
    pieces = []
    for h in range(4):
        codes = msg[h, 2, 0:1, :]
        low = codes < K2
        bucket = jnp.where(low, codes, codes - K2)
        sign = jnp.where(low, 1.0, -1.0)
        pieces.append(jnp.where(feature_bucket == bucket, sign, 0.0).astype(BF16))
    table_out = jnp.concatenate(pieces, axis=1)
    total = jnp.zeros((K1, 2 * K2), F32)
    for rb in range(4):
        gq = (acc[rb * 512 : (rb + 1) * 512, :] * SCORE).astype(BF16)
        hg = jnp.dot(table_out, gq, preferred_element_type=F32)
        high = hg.astype(BF16)
        rest = (hg - high.astype(F32)).astype(BF16)
        both = jnp.concatenate([high, rest], axis=0)
        total += lax.dot_general(
            jnp.concatenate([hit[rb, 0], hit[rb, 1]], axis=1), both, NT, preferred_element_type=F32
        )
    part[...] = total

    for i in range(1, RANKS):
        to = wrap(me + i, RANKS)
        rows = pl.ds(pl.multiple_of((to // 2) * 8, 8), 8)
        remote(part.at[rows, :], rs1.at[me], r1_ss, r1_rs, to).start()
    mine = pl.ds(pl.multiple_of((me // 2) * 8, 8), 8)
    pltpu.make_async_copy(part.at[mine, :], rs1.at[me], r1_rs).start()
    pltpu.make_async_copy(rs1, rs1, r1_rs).wait()
    summed = jnp.sum(rs1[...], axis=0)
    summed = (summed + pltpu.roll(summed, K2, 1)) * (SEQ * DIM // K1) ** -0.5
    summed = jnp.where(cc == 0, summed, pltpu.roll(summed, 4, 0))
    left = lax.broadcasted_iota(jnp.int32, (1, HD), 1) < K2
    first = jnp.where(left, summed[0:1, :], summed[1:2, :])
    second = jnp.where(left, summed[2:3, :], summed[3:4, :])
    sketch_out[...] = jnp.concatenate([first, second], axis=1)
    sk_send[...] = jnp.concatenate([first, second, jnp.zeros((6, HD), F32)], axis=0)

    for i in range(1, DOCS):
        pltpu.make_async_remote_copy(
            src_ref=sk_send, dst_ref=sk_all.at[doc], send_sem=ag_ss, recv_sem=ag_rs,
            device_id={"doc": wrap(doc + i, DOCS)}, device_id_type=pl.DeviceIdType.MESH,
        ).start()
    pltpu.make_async_copy(sk_send, sk_all.at[doc], ag_rs).start()
    pltpu.make_async_copy(sk_all, sk_all, ag_rs).wait()

    flat = sk_all[...].reshape(DOCS * 8, HD)
    stored = qs_ref[...].astype(F32)
    high = lax.Precision.HIGHEST
    even = lax.dot_general(stored[:, :HD], flat, NT, precision=high, preferred_element_type=F32)
    odd = lax.dot_general(stored[:, HD:], flat, NT, precision=high, preferred_element_type=F32)
    part2[...] = even + pltpu.roll(odd, HD - 1, 1)

    for i in range(1, RANKS):
        to = wrap(me + i, RANKS)
        rows = pl.ds(pl.multiple_of(to * 8, 8), 8)
        remote(part2.at[rows, :], rs2.at[me], r2_ss, r2_rs, to).start()
    mine = pl.ds(pl.multiple_of(me * 8, 8), 8)
    pltpu.make_async_copy(part2.at[mine, :], rs2.at[me], r2_rs).start()
    pltpu.make_async_copy(rs2, rs2, r2_rs).wait()
    totals = jnp.sum(rs2[...], axis=0) * (K1 * K2) ** -0.5
    pick = (
        lax.broadcasted_iota(jnp.int32, (DOCS, HD), 1)
        == 8 * lax.broadcasted_iota(jnp.int32, (DOCS, HD), 0)
    ).astype(F32)
    scores_out[...] = lax.dot_general(
        pick, totals, NT, precision=high, preferred_element_type=F32
    )

    done(kv.at[:, 0:3, 0], kx_ss)
    for i in range(4):
        msg_each(i, lambda c: c.wait_send())
    for slot in (0, 5, 6):
        q_left(slot)
    for dx in range(1, 4):
        hit_copy(dx).wait_send()
    hit_side().wait_send()

    z_each(lambda to, s: done(half(0, 0), z_ss.at[s]))

    @pl.when(zz == 1)
    def _():
        z_whole(0, 2, 1).wait_send()

    def s_done(i, _):
        s_copy(i).wait_send()
        return 0

    lax.fori_loop(0, zz + 1, s_done, 0)
    done(rs1.at[1:], r1_ss)
    done(sk_all.at[1:], ag_ss)
    done(rs2.at[1:], r2_ss)


def local(
    queries, key_heads, value_heads, out_grad, log_sums, row_delta, doc_start,
    layer_input, hash_in, hash_out, query_sketch,
):
    hbm = pl.BlockSpec(memory_space=pl.ANY)
    vmem = pl.BlockSpec(memory_space=pltpu.VMEM)
    smem = pl.BlockSpec(memory_space=pltpu.SMEM)
    dma = pltpu.SemaphoreType.DMA
    return pl.pallas_call(
        kernel,
        out_shape=(
            jax.ShapeDtypeStruct((1, 256), F32),
            jax.ShapeDtypeStruct((DOCS, 8), F32),
        ),
        in_specs=[hbm, hbm, hbm, hbm, vmem, vmem, smem, hbm, vmem, vmem, vmem],
        out_specs=(vmem, vmem),
        scratch_shapes=[
            pltpu.VMEM((2, 4, BLOCK, 512), BF16),
            pltpu.VMEM((2, 16, 2, ROWS, HD), BF16),
            pltpu.VMEM((2048, BLOCK), F32),
            pltpu.VMEM((ROWS, DIM), BF16),
            pltpu.VMEM((3, 32, HD), F32),
            pltpu.VMEM((4, 3, 8, HD), F32),
            pltpu.VMEM((K1, ROWS), BF16),
            pltpu.VMEM((4, 2, K1, ROWS), BF16),
            pltpu.VMEM((SEQ, HD), F32),
            pltpu.VMEM((K1, 2 * K2), F32),
            pltpu.VMEM((RANKS, 8, HD), F32),
            pltpu.VMEM((8, HD), F32),
            pltpu.VMEM((DOCS, 8, HD), F32),
            pltpu.VMEM((256, HD), F32),
            pltpu.VMEM((RANKS, 8, HD), F32),
            dma,
            dma((4,)), dma((4,)),
            dma, dma,
            dma((7,)), dma((4,)),
            dma((2,)), dma((4,)), dma((4,)), dma((4,)),
            dma((4,)), dma, dma, dma,
            dma, dma, dma, dma, dma, dma,
        ],
        compiler_params=pltpu.CompilerParams(
            collective_id=0, has_side_effects=True, vmem_limit_bytes=56 * 2**20
        ),
    )(
        queries, key_heads, value_heads, out_grad,
        log_sums.reshape(32, 128), row_delta.reshape(32, 128), doc_start, layer_input,
        hash_in.reshape(1, DIM), hash_out.reshape(1, HD), query_sketch,
    )


def solution(mesh):
    return jax.shard_map(
        local,
        mesh=mesh,
        in_specs=(
            P("doc", "ctx", None),
            P("doc", "ctx", None),
            P("doc", "ctx", None),
            P("doc", "ctx", None),
            P("doc", "ctx", None),
            P("doc", "ctx", None),
            P("doc"),
            P("doc", "ctx", None),
            P(),
            P("ctx"),
            P("doc", "ctx"),
        ),
        out_specs=(P("doc", "ctx"), P(None, ("doc", "ctx"))),
        check_vma=False,
    )
```

```python
import functools

import jax
import jax.numpy as jnp
from jax import lax
from jax.experimental import pallas as pl
from jax.experimental.pallas import tpu as pltpu
from jax.sharding import PartitionSpec as P

HD = 128
K1 = 128
K2 = 64
SEQ = 4096
DIM = 8192
DOCS = 16
RANKS = 32
ROWS = 128
BLOCK = 256
PLANE = 1024
LOG2E = 1.4426950408889634
SCORE = HD**-0.5
NEG = -1e30
NT = (((1,), (1,)), ((), ()))
TN = (((0,), (0,)), ((), ()))
F32 = jnp.float32
BF16 = jnp.bfloat16


def wrap(value, count):
    return jnp.where(value >= count, value - count, value)


def kernel(
    q_hbm, k_hbm, v_hbm, do_hbm, lse_ref, dl_ref, start_ref, x_hbm, hin_ref, hout_ref, qs_ref,
    sketch_out, scores_out,
    qd, kv, acc, xb, ld, msg, hit_own, hit, bias, part, rs1, sk_send, sk_all, part2, rs2,
    xsem, msg_ss, msg_rs, kx_ss, kx_rs, q_ss, q_rs, z_ss, z_rs, s_ss, s_rs,
    hi_ss, hi_rs, hs_ss, hs_rs, r1_ss, r1_rs, ag_ss, ag_rs, r2_ss, r2_rs,
):
    doc = lax.axis_index("doc")
    me = lax.axis_index("ctx")
    zz = me // 8
    in_plane = me - 8 * zz
    xx = in_plane // 2
    cc = in_plane - 2 * xx
    base = zz * 8
    sibling = me + 1 - 2 * cc

    def remote(src, dst, ss, rs, peer):
        return pltpu.make_async_remote_copy(
            src_ref=src, dst_ref=dst, send_sem=ss, recv_sem=rs,
            device_id={"ctx": peer}, device_id_type=pl.DeviceIdType.MESH,
        )

    def done(ref, sem):
        pltpu.make_async_copy(ref, ref, sem).wait()

    near_order = (4, 5, 3, 2, 6, 7, 1)
    ctx_peers = [
        wrap(zz + dz, 4) * 8 + wrap(in_plane + j, 8) for dz in (2, 1, 3) for j in (4, 5, 3, 2, 6, 7, 1, 0)
    ] + [base + wrap(in_plane + j, 8) for j in near_order]
    upper = doc // 8
    yy = doc - 8 * upper
    doc_peers = [(1 - upper) * 8 + wrap(yy + j, 8) for j in (4, 3, 5, 2, 6, 1, 7, 0)] + [
        upper * 8 + wrap(yy + j, 8) for j in (4, 3, 5, 2, 6, 1, 7)
    ]

    barrier = pltpu.get_barrier_semaphore()
    for peer in ctx_peers[:8]:
        pl.semaphore_signal(
            barrier, inc=1, device_id={"ctx": peer}, device_id_type=pl.DeviceIdType.MESH
        )
    for peer in doc_peers:
        pl.semaphore_signal(
            barrier, inc=1, device_id={"doc": peer}, device_id_type=pl.DeviceIdType.MESH
        )
    for peer in ctx_peers[8:]:
        pl.semaphore_signal(
            barrier, inc=1, device_id={"ctx": peer}, device_id_type=pl.DeviceIdType.MESH
        )
    x_copy = pltpu.make_async_copy(x_hbm.at[0], xb, xsem)
    x_copy.start()
    ld[0] = lse_ref[...] * LOG2E
    ld[1] = dl_ref[...]
    ld[2] = jnp.broadcast_to(hout_ref[...].astype(F32), (32, 128))
    pl.semaphore_wait(barrier, RANKS - 1 + DOCS - 1)

    def half(plane, core):
        return kv.at[:, pl.ds(plane * 4, 4), core]

    for dx in (1, 3, 2, 0):
        to = wrap(xx + dx, 4)
        lanes = pl.ds(pl.multiple_of(to * HD, HD), HD)
        for n, src in enumerate((k_hbm, v_hbm)):
            src = src.at[0, :, lanes]
            dst = kv.at[n, zz * 4 + xx, cc]
            if dx == 0:
                pltpu.make_async_copy(src, dst, kx_rs).start()
            else:
                remote(src, dst, kx_ss, kx_rs, base + 2 * to + cc).start()

    def z_each(go):
        @pl.when(zz < 3)
        def _():
            go(zz + 1, 0)

        @pl.when(zz == 0)
        def _():
            go(3, 1)

    def z_first(to, s):
        lanes = pl.ds(pl.multiple_of(xx * HD, HD), HD)
        for n, src in enumerate((k_hbm, v_hbm)):
            dst = kv.at[n, zz * 4 + xx, cc]
            remote(src.at[0, :, lanes], dst, z_ss.at[s], z_rs.at[zz], to * 8 + in_plane).start()

    z_each(z_first)

    @pl.when(zz == 0)
    def _():
        z_first(2, 2)

    rows = pl.ds(pl.multiple_of(cc * ROWS, ROWS), ROWS)

    def q_send(slot, dx, other):
        to = 2 * wrap(xx + dx, 4) + (1 - cc if other else cc)
        lanes = pl.ds(pl.multiple_of(to * 512, 512), 512)
        for n, src in enumerate((q_hbm, do_hbm)):
            src = src.at[0, :, lanes]
            dst = qd.at[n, xx, rows, :]
            if slot == 7:
                pltpu.make_async_copy(src, dst, q_rs.at[xx]).start()
            else:
                remote(src, dst, q_ss.at[slot], q_rs.at[xx], base + to).start()

    def q_left(slot):
        done(qd.at[:, 0, 0:ROWS, :], q_ss.at[slot])

    def q_arrive(rb):
        done(qd.at[:, rb], q_rs.at[rb])

    near = ((1, 1, 0), (2, 3, 0), (3, 1, 1), (4, 3, 1))
    q_send(0, 0, 1)
    for way in near:
        q_send(*way)
    q_send(7, 0, 0)

    own_head = zz * 2 + in_plane // 4
    head_slot = in_plane - 4 * (in_plane // 4)

    def msg_each(i, go):
        src, dst = ld.at[:, i * 8 : i * 8 + 8, :], msg.at[head_slot]
        peer = i * 8 + own_head

        @pl.when(peer != me)
        def _():
            go(remote(src, dst, msg_ss.at[i], msg_rs.at[head_slot], peer))

        return src, dst, peer

    for i in range(4):
        src, dst, peer = msg_each(i, lambda c: c.start())

        @pl.when(peer == me)
        def _():
            pltpu.make_async_copy(src, dst, msg_rs.at[head_slot]).start()

    def s_copy(plane):
        return remote(half(plane, cc), half(plane, cc), s_ss.at[plane], s_rs.at[plane], sibling)

    def z_block(dx, to, s):
        block = kv.at[:, zz * 4 + wrap(xx + dx, 4), cc]
        return remote(block, block, z_ss.at[s], z_rs.at[zz], to * 8 + in_plane)

    def z_send(to, s):
        for dx in (1, 3, 2):
            z_block(dx, to, s).start()

    done(half(zz, cc), kx_rs)
    z_each(z_send)
    s_copy(zz).start()

    def z_whole(plane, to, s):
        return remote(half(plane, cc), half(plane, cc), z_ss.at[s], z_rs.at[plane], to * 8 + in_plane)

    def z_arrive(plane):
        done(half(plane, cc), z_rs.at[plane])
        s_copy(plane).start()

    def s_arrive(plane):
        done(half(plane, 1 - cc), s_rs.at[plane])

    bias[...] = jnp.where(
        lax.broadcasted_iota(jnp.int32, (SEQ, HD), 0) >= start_ref[0], 0.0, NEG
    ).astype(F32)
    acc[...] = jnp.zeros_like(acc)

    x_copy.wait()
    bucket_of = lax.broadcasted_iota(jnp.int32, (K1, 1024), 0)

    def hash_step(j, total):
        cols = pl.ds(pl.multiple_of(j * 1024, 1024), 1024)
        codes = hin_ref[:, cols]
        low = codes < K1
        bucket = jnp.where(low, codes, codes - K1)
        sign = jnp.where(low, 1.0, -1.0)
        table = jnp.where(bucket_of == bucket, sign, 0.0).astype(BF16)
        return total + lax.dot_general(table, xb[:, cols], NT, preferred_element_type=F32)

    hit_own[...] = lax.fori_loop(0, DIM // 1024, hash_step, jnp.zeros((K1, ROWS), F32)).astype(BF16)

    def hit_copy(dx):
        to = base + 2 * wrap(xx + dx, 4) + cc
        return remote(hit_own, hit.at[xx, cc], hi_ss.at[dx], hi_rs, to)

    def hit_side():
        return remote(hit.at[:, cc], hit.at[:, cc], hs_ss, hs_rs, sibling)

    def front(rb, h, kk, vv):
        head = slice(h * HD, (h + 1) * HD)
        s = lax.dot_general(kk, qd[0, rb, :, head], NT, preferred_element_type=F32)
        gw = lax.dot_general(vv, qd[1, rb, :, head], NT, preferred_element_type=F32)
        return s, gw

    def back(rb, h, kk, low, s, gw, diagonal):
        count = kk.shape[0]
        lse = jnp.concatenate(
            [msg[h, 0, pl.ds(2 * rb, 1), :], msg[h, 0, pl.ds(2 * rb + 1, 1), :]], axis=1
        )
        delta = jnp.concatenate(
            [msg[h, 1, pl.ds(2 * rb, 1), :], msg[h, 1, pl.ds(2 * rb + 1, 1), :]], axis=1
        )
        x = s * (SCORE * LOG2E) - lse + jnp.concatenate([low, low], axis=1)
        p = jnp.exp2(x)
        if diagonal:
            seen = lax.broadcasted_iota(jnp.int32, (BLOCK, BLOCK), 0) <= lax.broadcasted_iota(
                jnp.int32, (BLOCK, BLOCK), 1
            )
            last = jnp.where(seen, p[count - BLOCK :], 0.0)
            p = last if count == BLOCK else jnp.concatenate([p[: count - BLOCK], last], axis=0)
        ds = (p * (gw - delta)).astype(BF16)
        r = lax.dot_general(kk, ds, TN, preferred_element_type=F32)
        rows = pl.ds(pl.multiple_of((rb * 4 + h) * HD, HD), HD)
        acc[rows, :] += r

    def attend(items, plane, chips, diagonal):
        count = chips * BLOCK
        blocks = pl.ds(plane * 4, chips)
        kk = kv[0, blocks].reshape(count, HD)
        vv = kv[1, blocks].reshape(count, HD)
        low = bias[pl.ds(pl.multiple_of(plane * PLANE, PLANE), count), :]
        now = front(*items[0], kk, vv)
        for n, item in enumerate(items):
            later = front(*items[n + 1], kk, vv) if n + 1 < len(items) else None
            back(*item, kk, low, *now, diagonal)
            now = later

    own, right, left, far = xx, wrap(xx + 1, 4), wrap(xx + 3, 4), wrap(xx + 2, 4)

    def diag(rb, picked):
        for r in range(4):

            @pl.when(rb == r)
            def _():
                attend([(r, h) for h in picked], zz, r + 1, True)

    def diag_whole(rb):
        q_arrive(rb)
        diag(rb, range(4))

    def diag_near():
        def step(i, _):
            diag_whole(jnp.where(i == 0, right, left))
            return 0

        lax.fori_loop(0, 2, step, 0)

    def whole(rb, plane):
        attend([(rb, h) for h in range(4)], plane, 4, False)

    def near_heads(plane):
        attend([(rb, h) for rb in (right, left) for h in range(4)], plane, 4, False)

    early = jnp.where(zz == 3, 2, jnp.where(zz >= 1, 1, 0))

    def each_early(go):
        def step(i, _):
            go(jnp.where(i == 0, zz - 1, 0))
            return 0

        lax.fori_loop(0, early, step, 0)

    for i in range(4):
        done(msg.at[i], msg_rs.at[i])
    s_arrive(zz)

    diag_whole(own)
    @pl.when(zz == 1)
    def _():
        done(half(0, 0), z_ss.at[0])
        z_whole(1, 3, 0).start()

    for way in near:
        q_left(way[0])
    q_send(5, 2, 0)
    q_send(6, 2, 1)
    diag_near()

    @pl.when(zz >= 1)
    def _():
        z_arrive(zz - 1)

    @pl.when(zz == 3)
    def _():
        z_arrive(0)
        for dx in (1, 3, 2):
            block = kv.at[:, wrap(xx + dx, 4), cc]
            remote(block, block, z_ss.at[1], z_rs.at[0], 16 + in_plane).start()

    def first_use(plane):
        s_arrive(plane)
        whole(own, plane)
        near_heads(plane)

    each_early(first_use)
    diag_whole(far)
    for dx in range(1, 4):
        hit_copy(dx).start()
    pltpu.make_async_copy(hit_own, hit.at[xx, cc], hi_rs).start()

    @pl.when(zz == 3)
    def _():
        z_arrive(1)

    each_early(lambda plane: whole(far, plane))
    done(hit.at[:, cc], hi_rs)
    hit_side().start()

    @pl.when(zz >= 2)
    def _():
        last = zz - 2

        @pl.when(zz == 2)
        def _():
            z_arrive(0)

        s_arrive(last)

        def step(rb, _):
            whole(rb, last)
            return 0

        lax.fori_loop(0, 4, step, 0)

    done(hit.at[:, 1 - cc], hs_rs)
    feature_bucket = lax.broadcasted_iota(jnp.int32, (K2, HD), 0).astype(F32)
    pieces = []
    for h in range(4):
        codes = msg[h, 2, 0:1, :]
        low = codes < K2
        bucket = jnp.where(low, codes, codes - K2)
        sign = jnp.where(low, 1.0, -1.0)
        pieces.append(jnp.where(feature_bucket == bucket, sign, 0.0).astype(BF16))
    table_out = jnp.concatenate(pieces, axis=1)
    total = jnp.zeros((K1, 2 * K2), F32)
    for rb in range(4):
        gq = (acc[rb * 512 : (rb + 1) * 512, :] * SCORE).astype(BF16)
        hg = jnp.dot(table_out, gq, preferred_element_type=F32)
        high = hg.astype(BF16)
        rest = (hg - high.astype(F32)).astype(BF16)
        both = jnp.concatenate([high, rest], axis=0)
        total += lax.dot_general(
            jnp.concatenate([hit[rb, 0], hit[rb, 1]], axis=1), both, NT, preferred_element_type=F32
        )
    part[...] = total

    for to in ctx_peers:
        rows = pl.ds(pl.multiple_of((to // 2) * 8, 8), 8)
        remote(part.at[rows, :], rs1.at[me], r1_ss, r1_rs, to).start()
    mine = pl.ds(pl.multiple_of((me // 2) * 8, 8), 8)
    pltpu.make_async_copy(part.at[mine, :], rs1.at[me], r1_rs).start()
    pltpu.make_async_copy(rs1, rs1, r1_rs).wait()
    summed = jnp.sum(rs1[...], axis=0)
    summed = (summed + pltpu.roll(summed, K2, 1)) * (SEQ * DIM // K1) ** -0.5
    summed = jnp.where(cc == 0, summed, pltpu.roll(summed, 4, 0))
    left = lax.broadcasted_iota(jnp.int32, (1, HD), 1) < K2
    first = jnp.where(left, summed[0:1, :], summed[1:2, :])
    second = jnp.where(left, summed[2:3, :], summed[3:4, :])
    sketch_out[...] = jnp.concatenate([first, second], axis=1)
    sk_send[...] = jnp.concatenate([first, second, jnp.zeros((6, HD), F32)], axis=0)

    for peer in doc_peers:
        pltpu.make_async_remote_copy(
            src_ref=sk_send, dst_ref=sk_all.at[doc], send_sem=ag_ss, recv_sem=ag_rs,
            device_id={"doc": peer}, device_id_type=pl.DeviceIdType.MESH,
        ).start()
    pltpu.make_async_copy(sk_send, sk_all.at[doc], ag_rs).start()
    pltpu.make_async_copy(sk_all, sk_all, ag_rs).wait()

    flat = sk_all[...].reshape(DOCS * 8, HD)
    stored = qs_ref[...].astype(F32)
    high = lax.Precision.HIGHEST
    even = lax.dot_general(stored[:, :HD], flat, NT, precision=high, preferred_element_type=F32)
    odd = lax.dot_general(stored[:, HD:], flat, NT, precision=high, preferred_element_type=F32)
    part2[...] = even + pltpu.roll(odd, HD - 1, 1)

    for to in ctx_peers:
        rows = pl.ds(pl.multiple_of(to * 8, 8), 8)
        remote(part2.at[rows, :], rs2.at[me], r2_ss, r2_rs, to).start()
    mine = pl.ds(pl.multiple_of(me * 8, 8), 8)
    pltpu.make_async_copy(part2.at[mine, :], rs2.at[me], r2_rs).start()
    pltpu.make_async_copy(rs2, rs2, r2_rs).wait()
    totals = jnp.sum(rs2[...], axis=0) * (K1 * K2) ** -0.5
    pick = (
        lax.broadcasted_iota(jnp.int32, (DOCS, HD), 1)
        == 8 * lax.broadcasted_iota(jnp.int32, (DOCS, HD), 0)
    ).astype(F32)
    scores_out[...] = lax.dot_general(
        pick, totals, NT, precision=high, preferred_element_type=F32
    )

    done(kv.at[:, 0:3, 0], kx_ss)
    for i in range(4):
        msg_each(i, lambda c: c.wait_send())
    for slot in (0, 5, 6):
        q_left(slot)
    for dx in range(1, 4):
        hit_copy(dx).wait_send()
    hit_side().wait_send()

    z_each(lambda to, s: done(half(0, 0), z_ss.at[s]))

    @pl.when(zz == 0)
    def _():
        done(kv.at[:, 0, 0], z_ss.at[2])

    @pl.when(zz == 3)
    def _():
        done(kv.at[:, 0:3, 0], z_ss.at[1])

    def s_done(i, _):
        s_copy(i).wait_send()
        return 0

    lax.fori_loop(0, zz + 1, s_done, 0)
    done(rs1.at[1:], r1_ss)
    done(sk_all.at[1:], ag_ss)
    done(rs2.at[1:], r2_ss)


def local(
    queries, key_heads, value_heads, out_grad, log_sums, row_delta, doc_start,
    layer_input, hash_in, hash_out, query_sketch,
):
    hbm = pl.BlockSpec(memory_space=pl.ANY)
    vmem = pl.BlockSpec(memory_space=pltpu.VMEM)
    smem = pl.BlockSpec(memory_space=pltpu.SMEM)
    dma = pltpu.SemaphoreType.DMA
    return pl.pallas_call(
        kernel,
        out_shape=(
            jax.ShapeDtypeStruct((1, 256), F32),
            jax.ShapeDtypeStruct((DOCS, 8), F32),
        ),
        in_specs=[hbm, hbm, hbm, hbm, vmem, vmem, smem, hbm, vmem, vmem, vmem],
        out_specs=(vmem, vmem),
        scratch_shapes=[
            pltpu.VMEM((2, 4, BLOCK, 512), BF16),
            pltpu.VMEM((2, 16, 2, ROWS, HD), BF16),
            pltpu.VMEM((2048, BLOCK), F32),
            pltpu.VMEM((ROWS, DIM), BF16),
            pltpu.VMEM((3, 32, HD), F32),
            pltpu.VMEM((4, 3, 8, HD), F32),
            pltpu.VMEM((K1, ROWS), BF16),
            pltpu.VMEM((4, 2, K1, ROWS), BF16),
            pltpu.VMEM((SEQ, HD), F32),
            pltpu.VMEM((K1, 2 * K2), F32),
            pltpu.VMEM((RANKS, 8, HD), F32),
            pltpu.VMEM((8, HD), F32),
            pltpu.VMEM((DOCS, 8, HD), F32),
            pltpu.VMEM((256, HD), F32),
            pltpu.VMEM((RANKS, 8, HD), F32),
            dma,
            dma((4,)), dma((4,)),
            dma, dma,
            dma((7,)), dma((4,)),
            dma((3,)), dma((4,)), dma((4,)), dma((4,)),
            dma((4,)), dma, dma, dma,
            dma, dma, dma, dma, dma, dma,
        ],
        compiler_params=pltpu.CompilerParams(
            collective_id=0, has_side_effects=True, vmem_limit_bytes=56 * 2**20
        ),
    )(
        queries, key_heads, value_heads, out_grad,
        log_sums.reshape(32, 128), row_delta.reshape(32, 128), doc_start, layer_input,
        hash_in.reshape(1, DIM), hash_out.reshape(1, HD), query_sketch,
    )


def solution(mesh):
    return jax.shard_map(
        local,
        mesh=mesh,
        in_specs=(
            P("doc", "ctx", None),
            P("doc", "ctx", None),
            P("doc", "ctx", None),
            P("doc", "ctx", None),
            P("doc", "ctx", None),
            P("doc", "ctx", None),
            P("doc"),
            P("doc", "ctx", None),
            P(),
            P("ctx"),
            P("doc", "ctx"),
        ),
        out_specs=(P("doc", "ctx"), P(None, ("doc", "ctx"))),
        check_vma=False,
    )
```

```python
import functools

import jax
import jax.numpy as jnp
from jax import lax
from jax.experimental import pallas as pl
from jax.experimental.pallas import tpu as pltpu
from jax.sharding import PartitionSpec as P

HD = 128
K1 = 128
K2 = 64
SEQ = 4096
DIM = 8192
DOCS = 16
RANKS = 32
ROWS = 128
BLOCK = 256
PLANE = 1024
LOG2E = 1.4426950408889634
SCORE = HD**-0.5
NEG = -1e30
NT = (((1,), (1,)), ((), ()))
TN = (((0,), (0,)), ((), ()))
F32 = jnp.float32
BF16 = jnp.bfloat16


def wrap(value, count):
    return jnp.where(value >= count, value - count, value)


def kernel(
    q_hbm, k_hbm, v_hbm, do_hbm, lse_ref, dl_ref, start_ref, x_hbm, hin_ref, hout_ref, qs_ref,
    sketch_out, scores_out,
    qd, kv, acc, xb, ld, msg, hit_own, hit, bias, part, rs1, sk_send, sk_all, part2, rs2, stage, stage_sem,
    xsem, msg_ss, msg_rs, kx_ss, kx_rs, q_ss, q_rs, z_ss, z_rs, s_ss, s_rs,
    hi_ss, hi_rs, hs_ss, hs_rs, r1_ss, r1_rs, ag_ss, ag_rs, r2_ss, r2_rs,
):
    doc = lax.axis_index("doc")
    me = lax.axis_index("ctx")
    zz = me // 8
    in_plane = me - 8 * zz
    xx = in_plane // 2
    cc = in_plane - 2 * xx
    base = zz * 8
    sibling = me + 1 - 2 * cc

    def remote(src, dst, ss, rs, peer):
        return pltpu.make_async_remote_copy(
            src_ref=src, dst_ref=dst, send_sem=ss, recv_sem=rs,
            device_id={"ctx": peer}, device_id_type=pl.DeviceIdType.MESH,
        )

    def done(ref, sem):
        pltpu.make_async_copy(ref, ref, sem).wait()

    near_order = (4, 5, 3, 2, 6, 7, 1)
    ctx_peers = [
        wrap(zz + dz, 4) * 8 + wrap(in_plane + j, 8) for dz in (2, 1, 3) for j in (4, 5, 3, 2, 6, 7, 1, 0)
    ] + [base + wrap(in_plane + j, 8) for j in near_order]
    upper = doc // 8
    yy = doc - 8 * upper
    doc_peers = [(1 - upper) * 8 + wrap(yy + j, 8) for j in (4, 3, 5, 2, 6, 1, 7, 0)] + [
        upper * 8 + wrap(yy + j, 8) for j in (4, 3, 5, 2, 6, 1, 7)
    ]

    barrier = pltpu.get_barrier_semaphore()
    for peer in ctx_peers[:8]:
        pl.semaphore_signal(
            barrier, inc=1, device_id={"ctx": peer}, device_id_type=pl.DeviceIdType.MESH
        )
    for peer in doc_peers:
        pl.semaphore_signal(
            barrier, inc=1, device_id={"doc": peer}, device_id_type=pl.DeviceIdType.MESH
        )
    for peer in ctx_peers[8:]:
        pl.semaphore_signal(
            barrier, inc=1, device_id={"ctx": peer}, device_id_type=pl.DeviceIdType.MESH
        )
    x_copy = pltpu.make_async_copy(x_hbm.at[0], xb, xsem)
    x_copy.start()
    stage_copies = [
        pltpu.make_async_copy(src.at[0], stage.at[n], stage_sem.at[n])
        for n, src in enumerate((q_hbm, do_hbm))
    ]
    for copy in stage_copies:
        copy.start()
    ld[0] = lse_ref[...] * LOG2E
    ld[1] = dl_ref[...]
    ld[2] = jnp.broadcast_to(hout_ref[...].astype(F32), (32, 128))
    pl.semaphore_wait(barrier, RANKS - 1 + DOCS - 1)

    def half(plane, core):
        return kv.at[:, pl.ds(plane * 4, 4), core]

    for dx in (1, 3, 2, 0):
        to = wrap(xx + dx, 4)
        lanes = pl.ds(pl.multiple_of(to * HD, HD), HD)
        for n, src in enumerate((k_hbm, v_hbm)):
            src = src.at[0, :, lanes]
            dst = kv.at[n, zz * 4 + xx, cc]
            if dx == 0:
                pltpu.make_async_copy(src, dst, kx_rs).start()
            else:
                remote(src, dst, kx_ss, kx_rs, base + 2 * to + cc).start()

    def z_each(go):
        @pl.when(zz < 3)
        def _():
            go(zz + 1, 0)

        @pl.when(zz == 0)
        def _():
            go(3, 1)

    def z_first(to, s):
        lanes = pl.ds(pl.multiple_of(xx * HD, HD), HD)
        for n, src in enumerate((k_hbm, v_hbm)):
            dst = kv.at[n, zz * 4 + xx, cc]
            remote(src.at[0, :, lanes], dst, z_ss.at[s], z_rs.at[zz], to * 8 + in_plane).start()

    z_each(z_first)

    @pl.when(zz == 0)
    def _():
        z_first(2, 2)

    rows = pl.ds(pl.multiple_of(cc * ROWS, ROWS), ROWS)

    def q_send(slot, dx, other):
        to = 2 * wrap(xx + dx, 4) + (1 - cc if other else cc)
        lanes = pl.ds(pl.multiple_of(to * 512, 512), 512)
        for n in range(2):
            src = stage.at[n, :, lanes]
            dst = qd.at[n, xx, rows, :]
            if slot == 7:
                pltpu.make_async_copy(src, dst, q_rs.at[xx]).start()
            else:
                remote(src, dst, q_ss.at[slot], q_rs.at[xx], base + to).start()

    def q_left(slot):
        done(qd.at[:, 0, 0:ROWS, :], q_ss.at[slot])

    def q_arrive(rb):
        done(qd.at[:, rb], q_rs.at[rb])

    near = ((1, 1, 0), (2, 3, 0), (3, 1, 1), (4, 3, 1))
    for copy in stage_copies:
        copy.wait()
    q_send(0, 0, 1)
    for way in near:
        q_send(*way)
    q_send(7, 0, 0)

    own_head = zz * 2 + in_plane // 4
    head_slot = in_plane - 4 * (in_plane // 4)

    def msg_each(i, go):
        src, dst = ld.at[:, i * 8 : i * 8 + 8, :], msg.at[head_slot]
        peer = i * 8 + own_head

        @pl.when(peer != me)
        def _():
            go(remote(src, dst, msg_ss.at[i], msg_rs.at[head_slot], peer))

        return src, dst, peer

    for i in range(4):
        src, dst, peer = msg_each(i, lambda c: c.start())

        @pl.when(peer == me)
        def _():
            pltpu.make_async_copy(src, dst, msg_rs.at[head_slot]).start()

    def s_copy(plane):
        return remote(half(plane, cc), half(plane, cc), s_ss.at[plane], s_rs.at[plane], sibling)

    def z_block(dx, to, s):
        block = kv.at[:, zz * 4 + wrap(xx + dx, 4), cc]
        return remote(block, block, z_ss.at[s], z_rs.at[zz], to * 8 + in_plane)

    def z_send(to, s):
        for dx in (1, 3, 2):
            z_block(dx, to, s).start()

    done(half(zz, cc), kx_rs)
    z_each(z_send)
    s_copy(zz).start()

    def z_whole(plane, to, s):
        return remote(half(plane, cc), half(plane, cc), z_ss.at[s], z_rs.at[plane], to * 8 + in_plane)

    def z_arrive(plane):
        done(half(plane, cc), z_rs.at[plane])
        s_copy(plane).start()

    def s_arrive(plane):
        done(half(plane, 1 - cc), s_rs.at[plane])

    bias[...] = jnp.where(
        lax.broadcasted_iota(jnp.int32, (SEQ, HD), 0) >= start_ref[0], 0.0, NEG
    ).astype(F32)
    acc[...] = jnp.zeros_like(acc)

    x_copy.wait()
    bucket_of = lax.broadcasted_iota(jnp.int32, (K1, 1024), 0)

    def hash_step(j, total):
        cols = pl.ds(pl.multiple_of(j * 1024, 1024), 1024)
        codes = hin_ref[:, cols]
        low = codes < K1
        bucket = jnp.where(low, codes, codes - K1)
        sign = jnp.where(low, 1.0, -1.0)
        table = jnp.where(bucket_of == bucket, sign, 0.0).astype(BF16)
        return total + lax.dot_general(table, xb[:, cols], NT, preferred_element_type=F32)

    hit_own[...] = lax.fori_loop(0, DIM // 1024, hash_step, jnp.zeros((K1, ROWS), F32)).astype(BF16)

    def hit_copy(dx):
        to = base + 2 * wrap(xx + dx, 4) + cc
        return remote(hit_own, hit.at[xx, cc], hi_ss.at[dx], hi_rs, to)

    def hit_side():
        return remote(hit.at[:, cc], hit.at[:, cc], hs_ss, hs_rs, sibling)

    def front(rb, h, kk, vv):
        head = slice(h * HD, (h + 1) * HD)
        s = lax.dot_general(kk, qd[0, rb, :, head], NT, preferred_element_type=F32)
        gw = lax.dot_general(vv, qd[1, rb, :, head], NT, preferred_element_type=F32)
        return s, gw

    def back(rb, h, kk, low, s, gw, diagonal):
        count = kk.shape[0]
        lse = jnp.concatenate(
            [msg[h, 0, pl.ds(2 * rb, 1), :], msg[h, 0, pl.ds(2 * rb + 1, 1), :]], axis=1
        )
        delta = jnp.concatenate(
            [msg[h, 1, pl.ds(2 * rb, 1), :], msg[h, 1, pl.ds(2 * rb + 1, 1), :]], axis=1
        )
        x = s * (SCORE * LOG2E) - lse + jnp.concatenate([low, low], axis=1)
        p = jnp.exp2(x)
        if diagonal:
            seen = lax.broadcasted_iota(jnp.int32, (BLOCK, BLOCK), 0) <= lax.broadcasted_iota(
                jnp.int32, (BLOCK, BLOCK), 1
            )
            last = jnp.where(seen, p[count - BLOCK :], 0.0)
            p = last if count == BLOCK else jnp.concatenate([p[: count - BLOCK], last], axis=0)
        ds = (p * (gw - delta)).astype(BF16)
        r = lax.dot_general(kk, ds, TN, preferred_element_type=F32)
        rows = pl.ds(pl.multiple_of((rb * 4 + h) * HD, HD), HD)
        acc[rows, :] += r

    def attend(items, plane, chips, diagonal):
        count = chips * BLOCK
        blocks = pl.ds(plane * 4, chips)
        kk = kv[0, blocks].reshape(count, HD)
        vv = kv[1, blocks].reshape(count, HD)
        low = bias[pl.ds(pl.multiple_of(plane * PLANE, PLANE), count), :]
        now = front(*items[0], kk, vv)
        for n, item in enumerate(items):
            later = front(*items[n + 1], kk, vv) if n + 1 < len(items) else None
            back(*item, kk, low, *now, diagonal)
            now = later

    own, right, left, far = xx, wrap(xx + 1, 4), wrap(xx + 3, 4), wrap(xx + 2, 4)

    def diag(rb, picked):
        for r in range(4):

            @pl.when(rb == r)
            def _():
                attend([(r, h) for h in picked], zz, r + 1, True)

    def diag_whole(rb):
        q_arrive(rb)
        diag(rb, range(4))

    def diag_near():
        def step(i, _):
            diag_whole(jnp.where(i == 0, right, left))
            return 0

        lax.fori_loop(0, 2, step, 0)

    def whole(rb, plane):
        attend([(rb, h) for h in range(4)], plane, 4, False)

    def near_heads(plane):
        attend([(rb, h) for rb in (right, left) for h in range(4)], plane, 4, False)

    early = jnp.where(zz == 3, 2, jnp.where(zz >= 1, 1, 0))

    def each_early(go):
        def step(i, _):
            go(jnp.where(i == 0, zz - 1, 0))
            return 0

        lax.fori_loop(0, early, step, 0)

    for i in range(4):
        done(msg.at[i], msg_rs.at[i])
    s_arrive(zz)

    diag_whole(own)
    @pl.when(zz == 1)
    def _():
        done(half(0, 0), z_ss.at[0])
        z_whole(1, 3, 0).start()

    for way in near:
        q_left(way[0])
    q_send(5, 2, 0)
    q_send(6, 2, 1)
    diag_near()

    @pl.when(zz >= 1)
    def _():
        z_arrive(zz - 1)

    @pl.when(zz == 3)
    def _():
        z_arrive(0)
        for dx in (1, 3, 2):
            block = kv.at[:, wrap(xx + dx, 4), cc]
            remote(block, block, z_ss.at[1], z_rs.at[0], 16 + in_plane).start()

    def first_use(plane):
        s_arrive(plane)
        whole(own, plane)
        near_heads(plane)

    each_early(first_use)
    diag_whole(far)
    for dx in range(1, 4):
        hit_copy(dx).start()
    pltpu.make_async_copy(hit_own, hit.at[xx, cc], hi_rs).start()

    @pl.when(zz == 3)
    def _():
        z_arrive(1)

    each_early(lambda plane: whole(far, plane))
    done(hit.at[:, cc], hi_rs)
    hit_side().start()

    @pl.when(zz >= 2)
    def _():
        last = zz - 2

        @pl.when(zz == 2)
        def _():
            z_arrive(0)

        s_arrive(last)

        def step(rb, _):
            whole(rb, last)
            return 0

        lax.fori_loop(0, 4, step, 0)

    done(hit.at[:, 1 - cc], hs_rs)
    feature_bucket = lax.broadcasted_iota(jnp.int32, (K2, HD), 0).astype(F32)
    pieces = []
    for h in range(4):
        codes = msg[h, 2, 0:1, :]
        low = codes < K2
        bucket = jnp.where(low, codes, codes - K2)
        sign = jnp.where(low, 1.0, -1.0)
        pieces.append(jnp.where(feature_bucket == bucket, sign, 0.0).astype(BF16))
    table_out = jnp.concatenate(pieces, axis=1)
    total = jnp.zeros((K1, 2 * K2), F32)
    for rb in range(4):
        gq = (acc[rb * 512 : (rb + 1) * 512, :] * SCORE).astype(BF16)
        hg = jnp.dot(table_out, gq, preferred_element_type=F32)
        high = hg.astype(BF16)
        rest = (hg - high.astype(F32)).astype(BF16)
        both = jnp.concatenate([high, rest], axis=0)
        total += lax.dot_general(
            jnp.concatenate([hit[rb, 0], hit[rb, 1]], axis=1), both, NT, preferred_element_type=F32
        )
    part[...] = total

    for to in ctx_peers:
        rows = pl.ds(pl.multiple_of((to // 2) * 8, 8), 8)
        remote(part.at[rows, :], rs1.at[me], r1_ss, r1_rs, to).start()
    mine = pl.ds(pl.multiple_of((me // 2) * 8, 8), 8)
    pltpu.make_async_copy(part.at[mine, :], rs1.at[me], r1_rs).start()
    pltpu.make_async_copy(rs1, rs1, r1_rs).wait()
    summed = jnp.sum(rs1[...], axis=0)
    summed = (summed + pltpu.roll(summed, K2, 1)) * (SEQ * DIM // K1) ** -0.5
    summed = jnp.where(cc == 0, summed, pltpu.roll(summed, 4, 0))
    left = lax.broadcasted_iota(jnp.int32, (1, HD), 1) < K2
    first = jnp.where(left, summed[0:1, :], summed[1:2, :])
    second = jnp.where(left, summed[2:3, :], summed[3:4, :])
    sketch_out[...] = jnp.concatenate([first, second], axis=1)
    sk_send[...] = jnp.concatenate([first, second, jnp.zeros((6, HD), F32)], axis=0)

    for peer in doc_peers:
        pltpu.make_async_remote_copy(
            src_ref=sk_send, dst_ref=sk_all.at[doc], send_sem=ag_ss, recv_sem=ag_rs,
            device_id={"doc": peer}, device_id_type=pl.DeviceIdType.MESH,
        ).start()
    pltpu.make_async_copy(sk_send, sk_all.at[doc], ag_rs).start()
    pltpu.make_async_copy(sk_all, sk_all, ag_rs).wait()

    flat = sk_all[...].reshape(DOCS * 8, HD)
    stored = qs_ref[...].astype(F32)
    high = lax.Precision.HIGHEST
    even = lax.dot_general(stored[:, :HD], flat, NT, precision=high, preferred_element_type=F32)
    odd = lax.dot_general(stored[:, HD:], flat, NT, precision=high, preferred_element_type=F32)
    part2[...] = even + pltpu.roll(odd, HD - 1, 1)

    for to in ctx_peers:
        rows = pl.ds(pl.multiple_of(to * 8, 8), 8)
        remote(part2.at[rows, :], rs2.at[me], r2_ss, r2_rs, to).start()
    mine = pl.ds(pl.multiple_of(me * 8, 8), 8)
    pltpu.make_async_copy(part2.at[mine, :], rs2.at[me], r2_rs).start()
    pltpu.make_async_copy(rs2, rs2, r2_rs).wait()
    totals = jnp.sum(rs2[...], axis=0) * (K1 * K2) ** -0.5
    pick = (
        lax.broadcasted_iota(jnp.int32, (DOCS, HD), 1)
        == 8 * lax.broadcasted_iota(jnp.int32, (DOCS, HD), 0)
    ).astype(F32)
    scores_out[...] = lax.dot_general(
        pick, totals, NT, precision=high, preferred_element_type=F32
    )

    done(kv.at[:, 0:3, 0], kx_ss)
    for i in range(4):
        msg_each(i, lambda c: c.wait_send())
    for slot in (0, 5, 6):
        q_left(slot)
    for dx in range(1, 4):
        hit_copy(dx).wait_send()
    hit_side().wait_send()

    z_each(lambda to, s: done(half(0, 0), z_ss.at[s]))

    @pl.when(zz == 0)
    def _():
        done(kv.at[:, 0, 0], z_ss.at[2])

    @pl.when(zz == 3)
    def _():
        done(kv.at[:, 0:3, 0], z_ss.at[1])

    def s_done(i, _):
        s_copy(i).wait_send()
        return 0

    lax.fori_loop(0, zz + 1, s_done, 0)
    done(rs1.at[1:], r1_ss)
    done(sk_all.at[1:], ag_ss)
    done(rs2.at[1:], r2_ss)


def local(
    queries, key_heads, value_heads, out_grad, log_sums, row_delta, doc_start,
    layer_input, hash_in, hash_out, query_sketch,
):
    hbm = pl.BlockSpec(memory_space=pl.ANY)
    vmem = pl.BlockSpec(memory_space=pltpu.VMEM)
    smem = pl.BlockSpec(memory_space=pltpu.SMEM)
    dma = pltpu.SemaphoreType.DMA
    return pl.pallas_call(
        kernel,
        out_shape=(
            jax.ShapeDtypeStruct((1, 256), F32),
            jax.ShapeDtypeStruct((DOCS, 8), F32),
        ),
        in_specs=[hbm, hbm, hbm, hbm, vmem, vmem, smem, hbm, vmem, vmem, vmem],
        out_specs=(vmem, vmem),
        scratch_shapes=[
            pltpu.VMEM((2, 4, BLOCK, 512), BF16),
            pltpu.VMEM((2, 16, 2, ROWS, HD), BF16),
            pltpu.VMEM((2048, BLOCK), F32),
            pltpu.VMEM((ROWS, DIM), BF16),
            pltpu.VMEM((3, 32, HD), F32),
            pltpu.VMEM((4, 3, 8, HD), F32),
            pltpu.VMEM((K1, ROWS), BF16),
            pltpu.VMEM((4, 2, K1, ROWS), BF16),
            pltpu.VMEM((SEQ, HD), F32),
            pltpu.VMEM((K1, 2 * K2), F32),
            pltpu.VMEM((RANKS, 8, HD), F32),
            pltpu.VMEM((8, HD), F32),
            pltpu.VMEM((DOCS, 8, HD), F32),
            pltpu.VMEM((256, HD), F32),
            pltpu.VMEM((RANKS, 8, HD), F32),
            pltpu.VMEM((2, ROWS, 4096), BF16), dma((2,)),
            dma,
            dma((4,)), dma((4,)),
            dma, dma,
            dma((7,)), dma((4,)),
            dma((3,)), dma((4,)), dma((4,)), dma((4,)),
            dma((4,)), dma, dma, dma,
            dma, dma, dma, dma, dma, dma,
        ],
        compiler_params=pltpu.CompilerParams(
            collective_id=0, has_side_effects=True, vmem_limit_bytes=56 * 2**20
        ),
    )(
        queries, key_heads, value_heads, out_grad,
        log_sums.reshape(32, 128), row_delta.reshape(32, 128), doc_start, layer_input,
        hash_in.reshape(1, DIM), hash_out.reshape(1, HD), query_sketch,
    )


def solution(mesh):
    return jax.shard_map(
        local,
        mesh=mesh,
        in_specs=(
            P("doc", "ctx", None),
            P("doc", "ctx", None),
            P("doc", "ctx", None),
            P("doc", "ctx", None),
            P("doc", "ctx", None),
            P("doc", "ctx", None),
            P("doc"),
            P("doc", "ctx", None),
            P(),
            P("ctx"),
            P("doc", "ctx"),
        ),
        out_specs=(P("doc", "ctx"), P(None, ("doc", "ctx"))),
        check_vma=False,
    )
```
